256 devices in a mesh: dp: 16 (over y_hi, z), mx: 8 (over x, core), my: 2 (over y_lo).
Axes of the slice: x: 4, y: 4 (y_hi: 2, y_lo: 2; y = y_hi * 2 + y_lo), z: 8, core: 2. Of those that a mesh axis runs over, the one named last changes fastest.
Arguments:
- inputs: bfloat16 [4096, 6144], P('dp', 'mx'), may hold values from -300 to 300
- ln_gain: float32 [6144], P('mx'), may hold values from 0.5 to 1.5
- w_qkv: bfloat16 [3, 6144, 4096], P(None, 'mx', 'my'), may hold values from -1 to 1
- qk_gain: float32 [2, 32, 128], P(None, ('my', 'mx')), may hold values from 0 to 8, as said below
- d_out: bfloat16 [4096, 4096], P('dp', ('my', 'mx')), may hold values from -110 to 110
Outputs:
- input_grad: bfloat16 [4096, 6144], P('dp', 'mx')
- w_grad: bfloat16 [3, 6144, 4096], P(None, ('mx', 'dp'), 'my')
- ln_gain_grad: float32 [6144], P('mx')
- qk_gain_grad: float32 [2, 32, 128], P(None, ('my', 'mx'))
The draws below stay inside these ranges and needn't reach their ends.
Inputs may be any that keep to these rules, and one draw needn't show every extreme that they name: `qk_gain`: positive.
All inputs are finite; a program needn't handle non-finite values.
Results may differ from the reference program's by a relative error of at most 0.015.
The reference program's roundings to bfloat16 on the way (of `scaled`, `projected`, `probs_low`, `d_values`, `d_scores` and `d_projected`) count: a program that leaves them out, or rounds other values in their place, can miss the bound.
Values may be sent and summed in bfloat16 or wider, within the bound.
A program may use at most 128 MiB of HBM per device.

```python
import math
import jax
import jax.numpy as jnp
from jax import lax

D = 6144
HD = 128
HW = 32
PATCH = 256
IMG_DEV = 1
IMAGES = 16
TOKENS = 4096
HQ = 4096
N_DP = 16


def draw_inputs(key, part):
    subkeys = jax.random.split(key, 3)
    sample = jnp.clip(jax.random.normal(subkeys[0], (TOKENS, D), jnp.float32), -4.0, 4.0)
    growth = 3.0 ** (jnp.arange(D, dtype=jnp.float32) / D)
    row_scale = jnp.exp(jax.random.uniform(subkeys[1], (TOKENS, 1), jnp.float32) * math.log(10.0))
    col_scale = jnp.exp(jax.random.uniform(subkeys[2], (1, D), jnp.float32) * math.log(3.5)) * growth[None, :]
    return (0.25 * sample * row_scale * col_scale).astype(jnp.bfloat16)


def draw_w_qkv(key, part):
    subkeys = jax.random.split(key, 3)
    query_part = jnp.clip(jax.random.normal(subkeys[0], (D, HQ), jnp.float32), -4.0, 4.0)
    key_part = jnp.clip(jax.random.normal(subkeys[1], (D, HQ), jnp.float32), -4.0, 4.0)
    value_part = jnp.clip(jax.random.normal(subkeys[2], (D, HQ), jnp.float32), -4.0, 4.0)
    stacked = jnp.stack([query_part, key_part, value_part]) / math.sqrt(D)
    return stacked.astype(jnp.bfloat16)


def draw_qk_gain(key, part):
    subkeys = jax.random.split(key, 2)
    head_scale = jnp.exp(jax.random.uniform(subkeys[0], (1, HW, 1), jnp.float32, math.log(0.5), math.log(2.0)))
    per_dim = 1.0 + 0.15 * jnp.clip(jax.random.normal(subkeys[1], (2, HW, HD), jnp.float32), -3.0, 3.0)
    return head_scale * per_dim


def draw_d_out(key, part):
    subkeys = jax.random.split(key, 2)
    sample = jnp.clip(jax.random.normal(subkeys[0], (TOKENS, HQ), jnp.float32), -4.0, 4.0)
    growth = 3.0 ** (jnp.arange(TOKENS, dtype=jnp.float32) / TOKENS)
    row_scale = jnp.exp(jax.random.uniform(subkeys[1], (TOKENS, 1), jnp.float32) * math.log(3.3))
    return (2.0 * sample * row_scale * growth[:, None]).astype(jnp.bfloat16)


def setup_inputs(seed: int = 0) -> dict:
    splits = jax.random.split(jax.random.key(seed), 6)
    return {
        "inputs": draw_inputs(jax.random.fold_in(splits[5], 71), 0),
        "ln_gain": jnp.clip(1.0 + 0.1 * jax.random.normal(splits[1], (D,), jnp.float32), 0.5, 1.5),
        "w_qkv": draw_w_qkv(jax.random.fold_in(splits[5], 71), 0),
        "qk_gain": draw_qk_gain(jax.random.fold_in(splits[5], 71), 0),
        "d_out": draw_d_out(jax.random.fold_in(splits[5], 71), 0),
    }


epsilon = 1e-06

def rounded(values):
    return lax.optimization_barrier(values.astype(jnp.bfloat16)).astype(jnp.float32)

def head_norm(values):
    average = lax.optimization_barrier(jnp.mean(values, axis=-1, keepdims=True))
    spread = lax.optimization_barrier(jnp.mean(values * values, axis=-1, keepdims=True)) - average * average
    inv_scale = lax.rsqrt(spread + epsilon)
    return ((values - average) * inv_scale, inv_scale)

def norm_back(d_normed, normed, inv_scale, gain_row):
    d_hat = d_normed * gain_row
    return inv_scale * (d_hat - lax.optimization_barrier(jnp.mean(d_hat, axis=-1, keepdims=True)) - normed * lax.optimization_barrier(jnp.mean(d_hat * normed, axis=-1, keepdims=True)))

def reference(inputs, ln_gain, w_qkv, qk_gain, d_out):
    widened = inputs.astype(jnp.float32)
    normed, inv_scale = head_norm(widened)
    scaled = (normed * ln_gain).astype(jnp.bfloat16)
    projected = jnp.stack([jnp.dot(scaled, w_qkv[proj_index], preferred_element_type=jnp.float32) for proj_index in range(3)])
    shaped = rounded(projected).reshape(3, IMAGES, PATCH, HW, HD)
    q_hat, q_inv = head_norm(shaped[0])
    k_hat, k_inv = head_norm(shaped[1])
    values = shaped[2]
    q_gain = qk_gain[0]
    k_gain = qk_gain[1]
    q_normed = rounded(q_hat * q_gain)
    k_normed = rounded(k_hat * k_gain)
    factor = 1.0 / math.sqrt(HD)
    scores = jnp.einsum('iphe,iqhe->ihpq', q_normed, k_normed) * factor
    row_max = lax.optimization_barrier(jnp.max(scores, axis=-1, keepdims=True))
    exponent = jnp.exp(scores - row_max)
    probabilities = exponent / lax.optimization_barrier(jnp.sum(exponent, axis=-1, keepdims=True))
    probs_low = rounded(probabilities)
    grad_heads = d_out.astype(jnp.float32).reshape(IMAGES, PATCH, HW, HD)
    d_values = jnp.einsum('ihpq,iphe->iqhe', probs_low, grad_heads).astype(jnp.bfloat16)
    d_probs = jnp.einsum('iphe,iqhe->ihpq', grad_heads, values)
    row_delta = lax.optimization_barrier(jnp.sum(probabilities * d_probs, axis=-1, keepdims=True))
    d_scores = rounded(probabilities * (d_probs - row_delta) * factor)
    d_qn = jnp.einsum('ihpq,iqhe->iphe', d_scores, k_normed)
    d_kn = jnp.einsum('ihpq,iphe->iqhe', d_scores, q_normed)
    qk_gain_grad = jnp.stack([lax.optimization_barrier(jnp.sum(d_qn * q_hat, axis=(0, 1))), lax.optimization_barrier(jnp.sum(d_kn * k_hat, axis=(0, 1)))])
    d_query = norm_back(d_qn, q_hat, q_inv, q_gain).astype(jnp.bfloat16)
    d_key = norm_back(d_kn, k_hat, k_inv, k_gain).astype(jnp.bfloat16)
    d_projected = jnp.stack([d_query, d_key, d_values]).reshape(3, TOKENS, HQ)
    d_scaled = jnp.dot(d_projected[0], w_qkv[0].T, preferred_element_type=jnp.float32)
    d_scaled = d_scaled + jnp.dot(d_projected[1], w_qkv[1].T, preferred_element_type=jnp.float32)
    d_scaled = d_scaled + jnp.dot(d_projected[2], w_qkv[2].T, preferred_element_type=jnp.float32)
    ln_gain_grad = lax.optimization_barrier(jnp.sum(d_scaled * normed, axis=0))
    input_grad = norm_back(d_scaled, normed, inv_scale, ln_gain).astype(jnp.bfloat16)
    group_rows = IMG_DEV * PATCH
    scaled_groups = scaled.reshape(N_DP, group_rows, D)
    grad_groups = d_projected.reshape(3, N_DP, group_rows, HQ)

    def add_group(group, running):
        block_x = lax.dynamic_index_in_dim(scaled_groups, group, 0, keepdims=False)
        block_g = lax.dynamic_index_in_dim(grad_groups, group, 1, keepdims=False)
        row_term = jnp.stack([jnp.dot(block_x.T, block_g[proj_index], preferred_element_type=jnp.float32) for proj_index in range(3)])
        return running + rounded(row_term)
    w_total = lax.fori_loop(0, N_DP, add_group, jnp.zeros((3, D, HQ), jnp.float32))
    return (input_grad, w_total.astype(jnp.bfloat16), ln_gain_grad, qk_gain_grad)
```

```python
import math

import jax
import jax.numpy as jnp
from jax import lax
from jax.sharding import PartitionSpec as P

PATCH = 256


epsilon = 1e-06


def head_norm(values):
    average = jnp.mean(values, axis=-1, keepdims=True)
    spread = jnp.mean(values * values, axis=-1, keepdims=True) - average * average
    inv_scale = lax.rsqrt(spread + epsilon)
    return ((values - average) * inv_scale, inv_scale)


def norm_back(d_normed, normed, inv_scale, gain_row):
    d_hat = d_normed * gain_row
    return inv_scale * (
        d_hat
        - jnp.mean(d_hat, axis=-1, keepdims=True)
        - normed * jnp.mean(d_hat * normed, axis=-1, keepdims=True)
    )


def body(inputs, ln_gain, w_qkv, qk_gain, d_out):
    token_rows = inputs.shape[0]
    width_local = inputs.shape[1]
    width = width_local * lax.axis_size("mx")
    widened = inputs.astype(jnp.float32)
    totals = lax.psum((jnp.sum(widened, axis=1), jnp.sum(widened * widened, axis=1)), "mx")
    average = totals[0][:, None] / width
    spread = totals[1][:, None] / width - average * average
    inv_scale = lax.rsqrt(spread + epsilon)
    normed = (widened - average) * inv_scale
    scaled = (normed * ln_gain[None, :]).astype(jnp.bfloat16)
    local_heads = qk_gain.shape[1]
    head_size = qk_gain.shape[2]
    group_heads = w_qkv.shape[2] // head_size
    weights = w_qkv.reshape(3, width_local, group_heads, head_size)
    projected = lax.psum_scatter(
        jnp.einsum("td,sdhe->hste", scaled, weights, preferred_element_type=jnp.float32),
        "mx",
        scatter_dimension=0,
        tiled=True,
    ).astype(jnp.bfloat16)
    images = token_rows // PATCH
    shaped = projected.reshape(local_heads, 3, images, PATCH, head_size)
    q_hat, q_inv = head_norm(shaped[:, 0].astype(jnp.float32))
    k_hat, k_inv = head_norm(shaped[:, 1].astype(jnp.float32))
    values = shaped[:, 2]
    q_gain = qk_gain[0][:, None, None, :]
    k_gain = qk_gain[1][:, None, None, :]
    q_normed = (q_hat * q_gain).astype(jnp.bfloat16)
    k_normed = (k_hat * k_gain).astype(jnp.bfloat16)
    factor = 1.0 / math.sqrt(head_size)
    scores = (
        jnp.einsum("hipe,hiqe->hipq", q_normed, k_normed, preferred_element_type=jnp.float32)
        * factor
    )
    row_max = jnp.max(scores, axis=-1, keepdims=True)
    exponent = jnp.exp(scores - row_max)
    probabilities = exponent / jnp.sum(exponent, axis=-1, keepdims=True)
    probs_low = probabilities.astype(jnp.bfloat16)
    grad_heads = (
        d_out.reshape(token_rows, local_heads, head_size)
        .transpose(1, 0, 2)
        .reshape(local_heads, images, PATCH, head_size)
    )
    d_values = jnp.einsum(
        "hipq,hipe->hiqe", probs_low, grad_heads, preferred_element_type=jnp.float32
    ).astype(jnp.bfloat16)
    d_probs = jnp.einsum("hipe,hiqe->hipq", grad_heads, values, preferred_element_type=jnp.float32)
    row_delta = jnp.sum(probabilities * d_probs, axis=-1, keepdims=True)
    d_scores = (probabilities * (d_probs - row_delta) * factor).astype(jnp.bfloat16)
    d_qn = jnp.einsum("hipq,hiqe->hipe", d_scores, k_normed, preferred_element_type=jnp.float32)
    d_kn = jnp.einsum("hipq,hipe->hiqe", d_scores, q_normed, preferred_element_type=jnp.float32)
    head_gain_part = jnp.stack(
        [jnp.sum(d_qn * q_hat, axis=(1, 2)), jnp.sum(d_kn * k_hat, axis=(1, 2))]
    )
    d_query = norm_back(d_qn, q_hat, q_inv, q_gain).astype(jnp.bfloat16)
    d_key = norm_back(d_kn, k_hat, k_inv, k_gain).astype(jnp.bfloat16)

    def head_rows(grads):
        return grads.reshape(local_heads, token_rows, head_size)

    block_rows = width_local // (lax.axis_size("dph") * lax.axis_size("dpz"))
    stacked = jnp.stack([head_rows(d_query), head_rows(d_key), head_rows(d_values)], axis=1)
    gathered = lax.all_gather(stacked, "mx", axis=0, tiled=True)
    d_scaled = jnp.einsum("hste,sdhe->td", gathered, weights, preferred_element_type=jnp.float32)
    feature_part = scaled
    w_part = jnp.einsum(
        "td,hste->dshe", feature_part, gathered, preferred_element_type=jnp.float32
    ).astype(jnp.bfloat16)
    w_half = lax.psum_scatter(w_part, "dph", scatter_dimension=0, tiled=True)
    w_rows = lax.psum_scatter(w_half, "dpz", scatter_dimension=0, tiled=True).astype(jnp.float32)
    w_grad = (
        w_rows.reshape(block_rows, 3, group_heads * head_size)
        .transpose(1, 0, 2)
        .astype(jnp.bfloat16)
    )
    gain_row = ln_gain[None, :]
    d_low = d_scaled.astype(jnp.bfloat16)
    d_other = lax.ppermute(d_low, "my", [(0, 1), (1, 0)])
    d_rows = d_low.astype(jnp.float32) + d_other.astype(jnp.float32)
    d_hat = d_rows * gain_row
    stat_sums = lax.psum((jnp.sum(d_hat, axis=1), jnp.sum(d_hat * normed, axis=1)), "mx")
    sum_first = stat_sums[0]
    sum_second = stat_sums[1]
    result_rows = (
        inv_scale * (d_hat - sum_first[:, None] / width - normed * sum_second[:, None] / width)
    ).astype(jnp.bfloat16)
    feature_part = jnp.sum(d_rows * normed, axis=0)
    head_total, feature_total = lax.psum((head_gain_part, feature_part), ("dph", "dpz"))
    return (result_rows, w_grad, feature_total, head_total)


def solution(mesh):
    dp = ("dph", "dpz")
    devices = mesh.devices.reshape(2, mesh.shape["dp"] // 2, mesh.shape["mx"], mesh.shape["my"])
    split_mesh = jax.sharding.Mesh(devices, ("dph", "dpz", "mx", "my"))
    in_specs = (
        P(dp, "mx"),
        P("mx"),
        P(None, "mx", "my"),
        P(None, ("my", "mx"), None),
        P(dp, ("my", "mx")),
    )
    out_specs = (P(dp, "mx"), P(None, ("mx",) + dp, "my"), P("mx"), P(None, ("my", "mx"), None))
    return jax.shard_map(body, mesh=split_mesh, in_specs=in_specs, out_specs=out_specs, check_vma=False)
```

```python
import math

import jax
import jax.numpy as jnp
from jax import lax
from jax.sharding import PartitionSpec as P

PATCH = 256
MX = ("mxx", "mxc")


epsilon = 1e-06


def head_norm(values):
    average = jnp.mean(values, axis=-1, keepdims=True)
    spread = jnp.mean(values * values, axis=-1, keepdims=True) - average * average
    inv_scale = lax.rsqrt(spread + epsilon)
    return ((values - average) * inv_scale, inv_scale)


def norm_back(d_normed, normed, inv_scale, gain_row):
    d_hat = d_normed * gain_row
    return inv_scale * (
        d_hat
        - jnp.mean(d_hat, axis=-1, keepdims=True)
        - normed * jnp.mean(d_hat * normed, axis=-1, keepdims=True)
    )


def body(inputs, ln_gain, w_qkv, qk_gain, d_out):
    token_rows = inputs.shape[0]
    width_local = inputs.shape[1]
    width = width_local * lax.axis_size(MX)
    widened = inputs.astype(jnp.float32)
    totals = lax.psum((jnp.sum(widened, axis=1), jnp.sum(widened * widened, axis=1)), MX)
    average = totals[0][:, None] / width
    spread = totals[1][:, None] / width - average * average
    inv_scale = lax.rsqrt(spread + epsilon)
    normed = (widened - average) * inv_scale
    scaled = (normed * ln_gain[None, :]).astype(jnp.bfloat16)
    local_heads = qk_gain.shape[1]
    head_size = qk_gain.shape[2]
    group_heads = w_qkv.shape[2] // head_size
    weights = w_qkv.reshape(3, width_local, group_heads, head_size)
    n_x = lax.axis_size("mxx")
    n_c = lax.axis_size("mxc")
    ordered = w_qkv.reshape(3, width_local, n_x, n_c, local_heads, head_size)
    partial = jnp.einsum("td,sdabje->bajste", scaled, ordered, preferred_element_type=jnp.float32)
    partial = partial.reshape(group_heads, 3, token_rows, head_size)
    projected = lax.psum_scatter(partial, "mxc", scatter_dimension=0, tiled=True)
    projected = lax.psum_scatter(projected, "mxx", scatter_dimension=0, tiled=True).astype(jnp.bfloat16)
    images = token_rows // PATCH
    shaped = projected.reshape(local_heads, 3, images, PATCH, head_size)
    q_hat, q_inv = head_norm(shaped[:, 0].astype(jnp.float32))
    k_hat, k_inv = head_norm(shaped[:, 1].astype(jnp.float32))
    values = shaped[:, 2]
    q_gain = qk_gain[0][:, None, None, :]
    k_gain = qk_gain[1][:, None, None, :]
    q_normed = (q_hat * q_gain).astype(jnp.bfloat16)
    k_normed = (k_hat * k_gain).astype(jnp.bfloat16)
    factor = 1.0 / math.sqrt(head_size)
    scores = (
        jnp.einsum("hipe,hiqe->hipq", q_normed, k_normed, preferred_element_type=jnp.float32)
        * factor
    )
    row_max = jnp.max(scores, axis=-1, keepdims=True)
    exponent = jnp.exp(scores - row_max)
    probabilities = exponent / jnp.sum(exponent, axis=-1, keepdims=True)
    probs_low = probabilities.astype(jnp.bfloat16)
    grad_heads = (
        d_out.reshape(token_rows, local_heads, head_size)
        .transpose(1, 0, 2)
        .reshape(local_heads, images, PATCH, head_size)
    )
    d_values = jnp.einsum(
        "hipq,hipe->hiqe", probs_low, grad_heads, preferred_element_type=jnp.float32
    ).astype(jnp.bfloat16)
    d_probs = jnp.einsum("hipe,hiqe->hipq", grad_heads, values, preferred_element_type=jnp.float32)
    row_delta = jnp.sum(probabilities * d_probs, axis=-1, keepdims=True)
    d_scores = (probabilities * (d_probs - row_delta) * factor).astype(jnp.bfloat16)
    d_qn = jnp.einsum("hipq,hiqe->hipe", d_scores, k_normed, preferred_element_type=jnp.float32)
    d_kn = jnp.einsum("hipq,hipe->hiqe", d_scores, q_normed, preferred_element_type=jnp.float32)
    head_gain_part = jnp.stack(
        [jnp.sum(d_qn * q_hat, axis=(1, 2)), jnp.sum(d_kn * k_hat, axis=(1, 2))]
    )
    d_query = norm_back(d_qn, q_hat, q_inv, q_gain).astype(jnp.bfloat16)
    d_key = norm_back(d_kn, k_hat, k_inv, k_gain).astype(jnp.bfloat16)

    def head_rows(grads):
        return grads.reshape(local_heads, token_rows, head_size)

    block_rows = width_local // (lax.axis_size("dph") * lax.axis_size("dpz"))
    stacked = jnp.stack([head_rows(d_query), head_rows(d_key), head_rows(d_values)], axis=1)
    gathered = lax.all_gather(stacked, MX, axis=0, tiled=True)
    d_scaled = jnp.einsum("hste,sdhe->td", gathered, weights, preferred_element_type=jnp.float32)
    feature_part = scaled
    n_hi = lax.axis_size("dph")
    n_z = lax.axis_size("dpz")
    feature_part = (
        feature_part.reshape(token_rows, n_hi, n_z, -1).transpose(0, 2, 1, 3).reshape(token_rows, -1)
    )
    w_part = jnp.einsum(
        "td,hste->dshe", feature_part, gathered, preferred_element_type=jnp.float32
    ).astype(jnp.bfloat16)
    w_half = lax.psum_scatter(w_part, "dpz", scatter_dimension=0, tiled=True)
    w_rows = lax.psum_scatter(w_half, "dph", scatter_dimension=0, tiled=True).astype(jnp.float32)
    w_grad = (
        w_rows.reshape(block_rows, 3, group_heads * head_size)
        .transpose(1, 0, 2)
        .astype(jnp.bfloat16)
    )
    gain_row = ln_gain[None, :]
    d_low = d_scaled.astype(jnp.bfloat16)
    d_other = lax.ppermute(d_low, "my", [(0, 1), (1, 0)])
    d_rows = d_low.astype(jnp.float32) + d_other.astype(jnp.float32)
    d_hat = d_rows * gain_row
    stat_sums = lax.psum((jnp.sum(d_hat, axis=1), jnp.sum(d_hat * normed, axis=1)), MX)
    sum_first = stat_sums[0]
    sum_second = stat_sums[1]
    result_rows = (
        inv_scale * (d_hat - sum_first[:, None] / width - normed * sum_second[:, None] / width)
    ).astype(jnp.bfloat16)
    feature_part = jnp.sum(d_rows * normed, axis=0)
    head_total, feature_total = lax.psum((head_gain_part, feature_part), ("dph", "dpz"))
    return (result_rows, w_grad, feature_total, head_total)


def solution(mesh):
    dp = ("dph", "dpz")
    devices = mesh.devices.reshape(2, mesh.shape["dp"] // 2, mesh.shape["mx"] // 2, 2, mesh.shape["my"])
    split_mesh = jax.sharding.Mesh(devices, ("dph", "dpz") + MX + ("my",))
    in_specs = (
        P(dp, MX),
        P(MX),
        P(None, MX, "my"),
        P(None, ("my",) + MX, None),
        P(dp, ("my",) + MX),
    )
    out_specs = (P(dp, MX), P(None, MX + dp, "my"), P(MX), P(None, ("my",) + MX, None))
    return jax.shard_map(body, mesh=split_mesh, in_specs=in_specs, out_specs=out_specs, check_vma=False)
```

```python
import math

import jax
import jax.numpy as jnp
from jax import lax
from jax.sharding import PartitionSpec as P

PATCH = 256


epsilon = 1e-06


def head_norm(values):
    average = jnp.mean(values, axis=-1, keepdims=True)
    spread = jnp.mean(values * values, axis=-1, keepdims=True) - average * average
    inv_scale = lax.rsqrt(spread + epsilon)
    return ((values - average) * inv_scale, inv_scale)


def norm_back(d_normed, normed, inv_scale, gain_row):
    d_hat = d_normed * gain_row
    return inv_scale * (
        d_hat
        - jnp.mean(d_hat, axis=-1, keepdims=True)
        - normed * jnp.mean(d_hat * normed, axis=-1, keepdims=True)
    )


def body(inputs, ln_gain, w_qkv, qk_gain, d_out):
    token_rows = inputs.shape[0]
    width_local = inputs.shape[1]
    width = width_local * lax.axis_size("mx")
    widened = inputs.astype(jnp.float32)
    totals = lax.psum((jnp.sum(widened, axis=1), jnp.sum(widened * widened, axis=1)), "mx")
    average = totals[0][:, None] / width
    spread = totals[1][:, None] / width - average * average
    inv_scale = lax.rsqrt(spread + epsilon)
    normed = (widened - average) * inv_scale
    scaled = (normed * ln_gain[None, :]).astype(jnp.bfloat16)
    local_heads = qk_gain.shape[1]
    head_size = qk_gain.shape[2]
    group_heads = w_qkv.shape[2] // head_size
    weights = w_qkv.reshape(3, width_local, group_heads, head_size)
    n_mx = lax.axis_size("mx")
    partial = jnp.einsum("td,sdhe->hste", scaled, weights, preferred_element_type=jnp.float32)
    pieces = lax.all_to_all(
        partial.astype(jnp.bfloat16).reshape(n_mx, local_heads, 3, token_rows, head_size),
        "mx",
        split_axis=0,
        concat_axis=0,
    )
    projected = jnp.sum(pieces.astype(jnp.float32), axis=0).astype(jnp.bfloat16)
    images = token_rows // PATCH
    shaped = projected.reshape(local_heads, 3, images, PATCH, head_size)
    q_hat, q_inv = head_norm(shaped[:, 0].astype(jnp.float32))
    k_hat, k_inv = head_norm(shaped[:, 1].astype(jnp.float32))
    values = shaped[:, 2]
    q_gain = qk_gain[0][:, None, None, :]
    k_gain = qk_gain[1][:, None, None, :]
    q_normed = (q_hat * q_gain).astype(jnp.bfloat16)
    k_normed = (k_hat * k_gain).astype(jnp.bfloat16)
    factor = 1.0 / math.sqrt(head_size)
    scores = (
        jnp.einsum("hipe,hiqe->hipq", q_normed, k_normed, preferred_element_type=jnp.float32)
        * factor
    )
    row_max = jnp.max(scores, axis=-1, keepdims=True)
    exponent = jnp.exp(scores - row_max)
    probabilities = exponent / jnp.sum(exponent, axis=-1, keepdims=True)
    probs_low = probabilities.astype(jnp.bfloat16)
    grad_heads = (
        d_out.reshape(token_rows, local_heads, head_size)
        .transpose(1, 0, 2)
        .reshape(local_heads, images, PATCH, head_size)
    )
    d_values = jnp.einsum(
        "hipq,hipe->hiqe", probs_low, grad_heads, preferred_element_type=jnp.float32
    ).astype(jnp.bfloat16)
    d_probs = jnp.einsum("hipe,hiqe->hipq", grad_heads, values, preferred_element_type=jnp.float32)
    row_delta = jnp.sum(probabilities * d_probs, axis=-1, keepdims=True)
    d_scores = (probabilities * (d_probs - row_delta) * factor).astype(jnp.bfloat16)
    d_qn = jnp.einsum("hipq,hiqe->hipe", d_scores, k_normed, preferred_element_type=jnp.float32)
    d_kn = jnp.einsum("hipq,hipe->hiqe", d_scores, q_normed, preferred_element_type=jnp.float32)
    head_gain_part = jnp.stack(
        [jnp.sum(d_qn * q_hat, axis=(1, 2)), jnp.sum(d_kn * k_hat, axis=(1, 2))]
    )
    d_query = norm_back(d_qn, q_hat, q_inv, q_gain).astype(jnp.bfloat16)
    d_key = norm_back(d_kn, k_hat, k_inv, k_gain).astype(jnp.bfloat16)

    def head_rows(grads):
        return grads.reshape(local_heads, token_rows, head_size)

    block_rows = width_local // (lax.axis_size("dph") * lax.axis_size("dpz"))
    stacked = jnp.stack([head_rows(d_query), head_rows(d_key), head_rows(d_values)], axis=1)
    gathered = lax.all_gather(stacked, "mx", axis=0, tiled=True)
    d_scaled = jnp.einsum("hste,sdhe->td", gathered, weights, preferred_element_type=jnp.float32)
    feature_part = scaled
    n_hi = lax.axis_size("dph")
    n_z = lax.axis_size("dpz")
    feature_part = (
        feature_part.reshape(token_rows, n_hi, n_z, -1).transpose(0, 2, 1, 3).reshape(token_rows, -1)
    )
    w_part = jnp.einsum(
        "td,hste->dshe", feature_part, gathered, preferred_element_type=jnp.float32
    ).astype(jnp.bfloat16)
    w_half = lax.psum_scatter(w_part, "dpz", scatter_dimension=0, tiled=True)
    gain_row = ln_gain[None, :]
    d_low = d_scaled.astype(jnp.bfloat16)
    d_other = lax.ppermute(d_low, "my", [(0, 1), (1, 0)])
    d_rows = d_low.astype(jnp.float32) + d_other.astype(jnp.float32)
    d_hat = d_rows * gain_row
    stat_sums = lax.psum((jnp.sum(d_hat, axis=1), jnp.sum(d_hat * normed, axis=1)), "mx")
    sum_first = stat_sums[0]
    sum_second = stat_sums[1]
    result_rows = (
        inv_scale * (d_hat - sum_first[:, None] / width - normed * sum_second[:, None] / width)
    ).astype(jnp.bfloat16)
    feature_part = jnp.sum(d_rows * normed, axis=0)
    head_total, feature_total = lax.psum((head_gain_part, feature_part), ("dph", "dpz"))
    w_half, result_rows, feature_total, head_total = lax.optimization_barrier(
        (w_half, result_rows, feature_total, head_total)
    )
    w_rows = lax.psum_scatter(w_half, "dph", scatter_dimension=0, tiled=True).astype(jnp.float32)
    w_grad = (
        w_rows.reshape(block_rows, 3, group_heads * head_size)
        .transpose(1, 0, 2)
        .astype(jnp.bfloat16)
    )
    return (result_rows, w_grad, feature_total, head_total)


def solution(mesh):
    dp = ("dph", "dpz")
    devices = mesh.devices.reshape(2, mesh.shape["dp"] // 2, mesh.shape["mx"], mesh.shape["my"])
    split_mesh = jax.sharding.Mesh(devices, ("dph", "dpz", "mx", "my"))
    in_specs = (
        P(dp, "mx"),
        P("mx"),
        P(None, "mx", "my"),
        P(None, ("my", "mx"), None),
        P(dp, ("my", "mx")),
    )
    out_specs = (P(dp, "mx"), P(None, ("mx",) + dp, "my"), P("mx"), P(None, ("my", "mx"), None))
    return jax.shard_map(body, mesh=split_mesh, in_specs=in_specs, out_specs=out_specs, check_vma=False)
```

```python
import math

import jax
import jax.numpy as jnp
from jax import lax
from jax.sharding import PartitionSpec as P

PATCH = 256


epsilon = 1e-06


def head_norm(values):
    average = jnp.mean(values, axis=-1, keepdims=True)
    spread = jnp.mean(values * values, axis=-1, keepdims=True) - average * average
    inv_scale = lax.rsqrt(spread + epsilon)
    return ((values - average) * inv_scale, inv_scale)


def norm_back(d_normed, normed, inv_scale, gain_row):
    d_hat = d_normed * gain_row
    return inv_scale * (
        d_hat
        - jnp.mean(d_hat, axis=-1, keepdims=True)
        - normed * jnp.mean(d_hat * normed, axis=-1, keepdims=True)
    )


def body(inputs, ln_gain, w_qkv, qk_gain, d_out):
    token_rows = inputs.shape[0]
    width_local = inputs.shape[1]
    width = width_local * lax.axis_size("mx")
    widened = inputs.astype(jnp.float32)
    totals = lax.psum((jnp.sum(widened, axis=1), jnp.sum(widened * widened, axis=1)), "mx")
    average = totals[0][:, None] / width
    spread = totals[1][:, None] / width - average * average
    inv_scale = lax.rsqrt(spread + epsilon)
    normed = (widened - average) * inv_scale
    scaled = (normed * ln_gain[None, :]).astype(jnp.bfloat16)
    local_heads = qk_gain.shape[1]
    head_size = qk_gain.shape[2]
    group_heads = w_qkv.shape[2] // head_size
    weights = w_qkv.reshape(3, width_local, group_heads, head_size)
    n_mx = lax.axis_size("mx")
    partial = jnp.einsum("td,sdhe->hste", scaled, weights, preferred_element_type=jnp.float32)
    pieces = lax.all_to_all(
        partial.reshape(n_mx, local_heads, 3, token_rows, head_size),
        "mx",
        split_axis=0,
        concat_axis=0,
    )
    projected = jnp.sum(pieces, axis=0).astype(jnp.bfloat16)
    images = token_rows // PATCH
    shaped = projected.reshape(local_heads, 3, images, PATCH, head_size)
    q_hat, q_inv = head_norm(shaped[:, 0].astype(jnp.float32))
    k_hat, k_inv = head_norm(shaped[:, 1].astype(jnp.float32))
    values = shaped[:, 2]
    q_gain = qk_gain[0][:, None, None, :]
    k_gain = qk_gain[1][:, None, None, :]
    q_normed = (q_hat * q_gain).astype(jnp.bfloat16)
    k_normed = (k_hat * k_gain).astype(jnp.bfloat16)
    factor = 1.0 / math.sqrt(head_size)
    scores = (
        jnp.einsum("hipe,hiqe->hipq", q_normed, k_normed, preferred_element_type=jnp.float32)
        * factor
    )
    row_max = jnp.max(scores, axis=-1, keepdims=True)
    exponent = jnp.exp(scores - row_max)
    probabilities = exponent / jnp.sum(exponent, axis=-1, keepdims=True)
    probs_low = probabilities.astype(jnp.bfloat16)
    grad_heads = (
        d_out.reshape(token_rows, local_heads, head_size)
        .transpose(1, 0, 2)
        .reshape(local_heads, images, PATCH, head_size)
    )
    d_values = jnp.einsum(
        "hipq,hipe->hiqe", probs_low, grad_heads, preferred_element_type=jnp.float32
    ).astype(jnp.bfloat16)
    d_probs = jnp.einsum("hipe,hiqe->hipq", grad_heads, values, preferred_element_type=jnp.float32)
    row_delta = jnp.sum(probabilities * d_probs, axis=-1, keepdims=True)
    d_scores = (probabilities * (d_probs - row_delta) * factor).astype(jnp.bfloat16)
    d_qn = jnp.einsum("hipq,hiqe->hipe", d_scores, k_normed, preferred_element_type=jnp.float32)
    d_kn = jnp.einsum("hipq,hipe->hiqe", d_scores, q_normed, preferred_element_type=jnp.float32)
    head_gain_part = jnp.stack(
        [jnp.sum(d_qn * q_hat, axis=(1, 2)), jnp.sum(d_kn * k_hat, axis=(1, 2))]
    )
    d_query = norm_back(d_qn, q_hat, q_inv, q_gain).astype(jnp.bfloat16)
    d_key = norm_back(d_kn, k_hat, k_inv, k_gain).astype(jnp.bfloat16)

    def head_rows(grads):
        return grads.reshape(local_heads, token_rows, head_size)

    block_rows = width_local // (lax.axis_size("dph") * lax.axis_size("dpz"))
    stacked = jnp.stack([head_rows(d_query), head_rows(d_key), head_rows(d_values)], axis=1)
    gathered = lax.all_gather(stacked, "mx", axis=0, tiled=True)
    d_scaled = jnp.einsum("hste,sdhe->td", gathered, weights, preferred_element_type=jnp.float32)
    feature_part = scaled
    n_hi = lax.axis_size("dph")
    n_z = lax.axis_size("dpz")
    feature_part = (
        feature_part.reshape(token_rows, n_hi, n_z, -1).transpose(0, 2, 1, 3).reshape(token_rows, -1)
    )
    w_part = jnp.einsum(
        "td,hste->dshe", feature_part, gathered, preferred_element_type=jnp.float32
    ).astype(jnp.bfloat16)
    w_half = lax.psum_scatter(w_part, "dpz", scatter_dimension=0, tiled=True)
    gain_row = ln_gain[None, :]
    d_low = d_scaled.astype(jnp.bfloat16)
    d_other = lax.ppermute(d_low, "my", [(0, 1), (1, 0)])
    d_rows = d_low.astype(jnp.float32) + d_other.astype(jnp.float32)
    d_hat = d_rows * gain_row
    stat_sums = lax.psum((jnp.sum(d_hat, axis=1), jnp.sum(d_hat * normed, axis=1)), "mx")
    sum_first = stat_sums[0]
    sum_second = stat_sums[1]
    result_rows = (
        inv_scale * (d_hat - sum_first[:, None] / width - normed * sum_second[:, None] / width)
    ).astype(jnp.bfloat16)
    feature_part = jnp.sum(d_rows * normed, axis=0)
    head_total, feature_total = lax.psum((head_gain_part, feature_part), ("dph", "dpz"))
    w_half, result_rows, feature_total, head_total = lax.optimization_barrier(
        (w_half, result_rows, feature_total, head_total)
    )
    w_rows = lax.psum_scatter(w_half, "dph", scatter_dimension=0, tiled=True).astype(jnp.float32)
    w_grad = (
        w_rows.reshape(block_rows, 3, group_heads * head_size)
        .transpose(1, 0, 2)
        .astype(jnp.bfloat16)
    )
    return (result_rows, w_grad, feature_total, head_total)


def solution(mesh):
    dp = ("dph", "dpz")
    devices = mesh.devices.reshape(2, mesh.shape["dp"] // 2, mesh.shape["mx"], mesh.shape["my"])
    split_mesh = jax.sharding.Mesh(devices, ("dph", "dpz", "mx", "my"))
    in_specs = (
        P(dp, "mx"),
        P("mx"),
        P(None, "mx", "my"),
        P(None, ("my", "mx"), None),
        P(dp, ("my", "mx")),
    )
    out_specs = (P(dp, "mx"), P(None, ("mx",) + dp, "my"), P("mx"), P(None, ("my", "mx"), None))
    return jax.shard_map(body, mesh=split_mesh, in_specs=in_specs, out_specs=out_specs, check_vma=False)
```

```python
import math

import jax
import jax.numpy as jnp
from jax import lax
from jax.sharding import PartitionSpec as P

PATCH = 256


epsilon = 1e-06


def head_norm(values):
    average = jnp.mean(values, axis=-1, keepdims=True)
    spread = jnp.mean(values * values, axis=-1, keepdims=True) - average * average
    inv_scale = lax.rsqrt(spread + epsilon)
    return ((values - average) * inv_scale, inv_scale)


def norm_back(d_normed, normed, inv_scale, gain_row):
    d_hat = d_normed * gain_row
    return inv_scale * (
        d_hat
        - jnp.mean(d_hat, axis=-1, keepdims=True)
        - normed * jnp.mean(d_hat * normed, axis=-1, keepdims=True)
    )


def body(inputs, ln_gain, w_qkv, qk_gain, d_out):
    token_rows = inputs.shape[0]
    width_local = inputs.shape[1]
    width = width_local * lax.axis_size("mx")
    widened = inputs.astype(jnp.float32)
    totals = lax.psum((jnp.sum(widened, axis=1), jnp.sum(widened * widened, axis=1)), "mx")
    average = totals[0][:, None] / width
    spread = totals[1][:, None] / width - average * average
    inv_scale = lax.rsqrt(spread + epsilon)
    normed = (widened - average) * inv_scale
    scaled = (normed * ln_gain[None, :]).astype(jnp.bfloat16)
    local_heads = qk_gain.shape[1]
    head_size = qk_gain.shape[2]
    group_heads = w_qkv.shape[2] // head_size
    weights = w_qkv.reshape(3, width_local, group_heads, head_size)
    n_mx = lax.axis_size("mx")
    partial = jnp.einsum("td,sdhe->hste", scaled, weights, preferred_element_type=jnp.float32)
    partial = partial.reshape(n_mx, local_heads, 3, token_rows, head_size)
    qk_pieces = lax.all_to_all(partial[:, :, :2], "mx", split_axis=0, concat_axis=0)
    v_pieces = lax.all_to_all(partial[:, :, 2:].astype(jnp.bfloat16), "mx", split_axis=0, concat_axis=0)
    projected = jnp.concatenate(
        [jnp.sum(qk_pieces, axis=0), jnp.sum(v_pieces.astype(jnp.float32), axis=0)], axis=1
    ).astype(jnp.bfloat16)
    images = token_rows // PATCH
    shaped = projected.reshape(local_heads, 3, images, PATCH, head_size)
    q_hat, q_inv = head_norm(shaped[:, 0].astype(jnp.float32))
    k_hat, k_inv = head_norm(shaped[:, 1].astype(jnp.float32))
    values = shaped[:, 2]
    q_gain = qk_gain[0][:, None, None, :]
    k_gain = qk_gain[1][:, None, None, :]
    q_normed = (q_hat * q_gain).astype(jnp.bfloat16)
    k_normed = (k_hat * k_gain).astype(jnp.bfloat16)
    factor = 1.0 / math.sqrt(head_size)
    scores = (
        jnp.einsum("hipe,hiqe->hipq", q_normed, k_normed, preferred_element_type=jnp.float32)
        * factor
    )
    row_max = jnp.max(scores, axis=-1, keepdims=True)
    exponent = jnp.exp(scores - row_max)
    probabilities = exponent / jnp.sum(exponent, axis=-1, keepdims=True)
    probs_low = probabilities.astype(jnp.bfloat16)
    grad_heads = (
        d_out.reshape(token_rows, local_heads, head_size)
        .transpose(1, 0, 2)
        .reshape(local_heads, images, PATCH, head_size)
    )
    d_values = jnp.einsum(
        "hipq,hipe->hiqe", probs_low, grad_heads, preferred_element_type=jnp.float32
    ).astype(jnp.bfloat16)
    d_probs = jnp.einsum("hipe,hiqe->hipq", grad_heads, values, preferred_element_type=jnp.float32)
    row_delta = jnp.sum(probabilities * d_probs, axis=-1, keepdims=True)
    d_scores = (probabilities * (d_probs - row_delta) * factor).astype(jnp.bfloat16)
    d_qn = jnp.einsum("hipq,hiqe->hipe", d_scores, k_normed, preferred_element_type=jnp.float32)
    d_kn = jnp.einsum("hipq,hipe->hiqe", d_scores, q_normed, preferred_element_type=jnp.float32)
    head_gain_part = jnp.stack(
        [jnp.sum(d_qn * q_hat, axis=(1, 2)), jnp.sum(d_kn * k_hat, axis=(1, 2))]
    )
    d_query = norm_back(d_qn, q_hat, q_inv, q_gain).astype(jnp.bfloat16)
    d_key = norm_back(d_kn, k_hat, k_inv, k_gain).astype(jnp.bfloat16)

    def head_rows(grads):
        return grads.reshape(local_heads, token_rows, head_size)

    block_rows = width_local // (lax.axis_size("dph") * lax.axis_size("dpz"))
    stacked = jnp.stack([head_rows(d_query), head_rows(d_key), head_rows(d_values)], axis=1)
    gathered = lax.all_gather(stacked, "mx", axis=0, tiled=True)
    d_scaled = jnp.einsum("hste,sdhe->td", gathered, weights, preferred_element_type=jnp.float32)
    feature_part = scaled
    n_hi = lax.axis_size("dph")
    n_z = lax.axis_size("dpz")
    feature_part = (
        feature_part.reshape(token_rows, n_hi, n_z, -1).transpose(0, 2, 1, 3).reshape(token_rows, -1)
    )
    w_part = jnp.einsum(
        "td,hste->dshe", feature_part, gathered, preferred_element_type=jnp.float32
    ).astype(jnp.bfloat16)
    w_half = lax.psum_scatter(w_part, "dpz", scatter_dimension=0, tiled=True)
    gain_row = ln_gain[None, :]
    d_low = d_scaled.astype(jnp.bfloat16)
    d_other = lax.ppermute(d_low, "my", [(0, 1), (1, 0)])
    d_rows = d_low.astype(jnp.float32) + d_other.astype(jnp.float32)
    d_hat = d_rows * gain_row
    stat_sums = lax.psum((jnp.sum(d_hat, axis=1), jnp.sum(d_hat * normed, axis=1)), "mx")
    sum_first = stat_sums[0]
    sum_second = stat_sums[1]
    result_rows = (
        inv_scale * (d_hat - sum_first[:, None] / width - normed * sum_second[:, None] / width)
    ).astype(jnp.bfloat16)
    feature_part = jnp.sum(d_rows * normed, axis=0)
    head_total, feature_total = lax.psum((head_gain_part, feature_part), ("dph", "dpz"))
    w_half, result_rows, feature_total, head_total = lax.optimization_barrier(
        (w_half, result_rows, feature_total, head_total)
    )
    w_rows = lax.psum_scatter(w_half, "dph", scatter_dimension=0, tiled=True).astype(jnp.float32)
    w_grad = (
        w_rows.reshape(block_rows, 3, group_heads * head_size)
        .transpose(1, 0, 2)
        .astype(jnp.bfloat16)
    )
    return (result_rows, w_grad, feature_total, head_total)


def solution(mesh):
    dp = ("dph", "dpz")
    devices = mesh.devices.reshape(2, mesh.shape["dp"] // 2, mesh.shape["mx"], mesh.shape["my"])
    split_mesh = jax.sharding.Mesh(devices, ("dph", "dpz", "mx", "my"))
    in_specs = (
        P(dp, "mx"),
        P("mx"),
        P(None, "mx", "my"),
        P(None, ("my", "mx"), None),
        P(dp, ("my", "mx")),
    )
    out_specs = (P(dp, "mx"), P(None, ("mx",) + dp, "my"), P("mx"), P(None, ("my", "mx"), None))
    return jax.shard_map(body, mesh=split_mesh, in_specs=in_specs, out_specs=out_specs, check_vma=False)
```

```python
import math

import jax
import jax.numpy as jnp
from jax import lax
from jax.sharding import PartitionSpec as P

PATCH = 256


epsilon = 1e-06


def head_norm(values):
    average = jnp.mean(values, axis=-1, keepdims=True)
    spread = jnp.mean(values * values, axis=-1, keepdims=True) - average * average
    inv_scale = lax.rsqrt(spread + epsilon)
    return ((values - average) * inv_scale, inv_scale)


def norm_back(d_normed, normed, inv_scale, gain_row):
    d_hat = d_normed * gain_row
    return inv_scale * (
        d_hat
        - jnp.mean(d_hat, axis=-1, keepdims=True)
        - normed * jnp.mean(d_hat * normed, axis=-1, keepdims=True)
    )


def body(inputs, ln_gain, w_qkv, qk_gain, d_out):
    token_rows = inputs.shape[0]
    width_local = inputs.shape[1]
    width = width_local * lax.axis_size("mx")
    widened = inputs.astype(jnp.float32)
    totals = lax.psum((jnp.sum(widened, axis=1), jnp.sum(widened * widened, axis=1)), "mx")
    average = totals[0][:, None] / width
    spread = totals[1][:, None] / width - average * average
    inv_scale = lax.rsqrt(spread + epsilon)
    normed = (widened - average) * inv_scale
    scaled = (normed * ln_gain[None, :]).astype(jnp.bfloat16)
    local_heads = qk_gain.shape[1]
    head_size = qk_gain.shape[2]
    group_heads = w_qkv.shape[2] // head_size
    weights = w_qkv.reshape(3, width_local, group_heads, head_size)
    n_mx = lax.axis_size("mx")
    partial = jnp.einsum("td,sdhe->hste", scaled, weights, preferred_element_type=jnp.float32)
    partial = partial.reshape(n_mx, local_heads, 3, token_rows, head_size)
    qk_pieces = lax.all_to_all(partial[:, :, :2], "mx", split_axis=0, concat_axis=0)
    v_pieces = lax.all_to_all(partial[:, :, 2:].astype(jnp.bfloat16), "mx", split_axis=0, concat_axis=0)
    projected = jnp.concatenate(
        [jnp.sum(qk_pieces, axis=0), jnp.sum(v_pieces.astype(jnp.float32), axis=0)], axis=1
    ).astype(jnp.bfloat16)
    images = token_rows // PATCH
    shaped = projected.reshape(local_heads, 3, images, PATCH, head_size)
    q_hat, q_inv = head_norm(shaped[:, 0].astype(jnp.float32))
    k_hat, k_inv = head_norm(shaped[:, 1].astype(jnp.float32))
    values = shaped[:, 2]
    q_gain = qk_gain[0][:, None, None, :]
    k_gain = qk_gain[1][:, None, None, :]
    q_normed = (q_hat * q_gain).astype(jnp.bfloat16)
    k_normed = (k_hat * k_gain).astype(jnp.bfloat16)
    factor = 1.0 / math.sqrt(head_size)
    scores = (
        jnp.einsum("hipe,hiqe->hipq", q_normed, k_normed, preferred_element_type=jnp.float32)
        * factor
    )
    row_max = jnp.max(scores, axis=-1, keepdims=True)
    exponent = jnp.exp(scores - row_max)
    probabilities = exponent / jnp.sum(exponent, axis=-1, keepdims=True)
    probs_low = probabilities.astype(jnp.bfloat16)
    grad_heads = (
        d_out.reshape(token_rows, local_heads, head_size)
        .transpose(1, 0, 2)
        .reshape(local_heads, images, PATCH, head_size)
    )
    d_values = jnp.einsum(
        "hipq,hipe->hiqe", probs_low, grad_heads, preferred_element_type=jnp.float32
    ).astype(jnp.bfloat16)
    d_probs = jnp.einsum("hipe,hiqe->hipq", grad_heads, values, preferred_element_type=jnp.float32)
    row_delta = jnp.sum(probabilities * d_probs, axis=-1, keepdims=True)
    d_scores = (probabilities * (d_probs - row_delta) * factor).astype(jnp.bfloat16)
    d_qn = jnp.einsum("hipq,hiqe->hipe", d_scores, k_normed, preferred_element_type=jnp.float32)
    d_kn = jnp.einsum("hipq,hipe->hiqe", d_scores, q_normed, preferred_element_type=jnp.float32)
    head_gain_part = jnp.stack(
        [jnp.sum(d_qn * q_hat, axis=(1, 2)), jnp.sum(d_kn * k_hat, axis=(1, 2))]
    )
    d_query = norm_back(d_qn, q_hat, q_inv, q_gain).astype(jnp.bfloat16)
    d_key = norm_back(d_kn, k_hat, k_inv, k_gain).astype(jnp.bfloat16)

    def head_rows(grads):
        return grads.reshape(local_heads, token_rows, head_size)

    block_rows = width_local // (lax.axis_size("dph") * lax.axis_size("dpz"))
    stacked = jnp.stack([head_rows(d_query), head_rows(d_key), head_rows(d_values)], axis=1)
    gathered = lax.all_gather(stacked, "mx", axis=0, tiled=True)
    d_scaled = jnp.einsum("hste,sdhe->td", gathered, weights, preferred_element_type=jnp.float32)
    feature_part = scaled
    n_hi = lax.axis_size("dph")
    n_z = lax.axis_size("dpz")
    z_first = (
        feature_part.reshape(token_rows, n_hi, n_z, -1).transpose(0, 2, 1, 3).reshape(token_rows, -1)
    )
    split = group_heads // 2
    w_part = jnp.einsum(
        "td,hste->dshe", z_first, gathered[:split], preferred_element_type=jnp.float32
    ).astype(jnp.bfloat16)
    w_other = jnp.einsum(
        "td,hste->dshe", feature_part, gathered[split:], preferred_element_type=jnp.float32
    ).astype(jnp.bfloat16)
    hi_rows = w_other.reshape(n_hi, width_local // n_hi, 3, group_heads - split, head_size)
    hi_index = lax.axis_index("dph")
    swapped = lax.ppermute(hi_rows[1 - hi_index], "dph", [(0, 1), (1, 0)])
    w_half = lax.psum_scatter(w_part, "dpz", scatter_dimension=0, tiled=True)
    gain_row = ln_gain[None, :]
    d_low = d_scaled.astype(jnp.bfloat16)
    d_other = lax.ppermute(d_low, "my", [(0, 1), (1, 0)])
    d_rows = d_low.astype(jnp.float32) + d_other.astype(jnp.float32)
    d_hat = d_rows * gain_row
    stat_sums = lax.psum((jnp.sum(d_hat, axis=1), jnp.sum(d_hat * normed, axis=1)), "mx")
    sum_first = stat_sums[0]
    sum_second = stat_sums[1]
    result_rows = (
        inv_scale * (d_hat - sum_first[:, None] / width - normed * sum_second[:, None] / width)
    ).astype(jnp.bfloat16)
    feature_part = jnp.sum(d_rows * normed, axis=0)
    head_total, feature_total = lax.psum((head_gain_part, feature_part), ("dph", "dpz"))
    w_half, swapped, result_rows, feature_total, head_total = lax.optimization_barrier(
        (w_half, swapped, result_rows, feature_total, head_total)
    )
    hi_sum = (hi_rows[hi_index].astype(jnp.float32) + swapped.astype(jnp.float32)).astype(jnp.bfloat16)
    w_late = lax.psum_scatter(hi_sum, "dpz", scatter_dimension=0, tiled=True)
    w_rows = lax.psum_scatter(w_half, "dph", scatter_dimension=0, tiled=True)
    w_rows = jnp.concatenate([w_rows, w_late], axis=2).astype(jnp.float32)
    w_grad = (
        w_rows.reshape(block_rows, 3, group_heads * head_size)
        .transpose(1, 0, 2)
        .astype(jnp.bfloat16)
    )
    return (result_rows, w_grad, feature_total, head_total)


def solution(mesh):
    dp = ("dph", "dpz")
    devices = mesh.devices.reshape(2, mesh.shape["dp"] // 2, mesh.shape["mx"], mesh.shape["my"])
    split_mesh = jax.sharding.Mesh(devices, ("dph", "dpz", "mx", "my"))
    in_specs = (
        P(dp, "mx"),
        P("mx"),
        P(None, "mx", "my"),
        P(None, ("my", "mx"), None),
        P(dp, ("my", "mx")),
    )
    out_specs = (P(dp, "mx"), P(None, ("mx",) + dp, "my"), P("mx"), P(None, ("my", "mx"), None))
    return jax.shard_map(body, mesh=split_mesh, in_specs=in_specs, out_specs=out_specs, check_vma=False)
```

```python
import math

import jax
import jax.numpy as jnp
from jax import lax
from jax.sharding import PartitionSpec as P

PATCH = 256
MX = ("mxx", "mxc")


epsilon = 1e-06


def head_norm(values):
    average = jnp.mean(values, axis=-1, keepdims=True)
    spread = jnp.mean(values * values, axis=-1, keepdims=True) - average * average
    inv_scale = lax.rsqrt(spread + epsilon)
    return ((values - average) * inv_scale, inv_scale)


def norm_back(d_normed, normed, inv_scale, gain_row):
    d_hat = d_normed * gain_row
    return inv_scale * (
        d_hat
        - jnp.mean(d_hat, axis=-1, keepdims=True)
        - normed * jnp.mean(d_hat * normed, axis=-1, keepdims=True)
    )


def body(inputs, ln_gain, w_qkv, qk_gain, d_out):
    token_rows = inputs.shape[0]
    width_local = inputs.shape[1]
    width = width_local * lax.axis_size(MX)
    widened = inputs.astype(jnp.float32)
    totals = lax.psum((jnp.sum(widened, axis=1), jnp.sum(widened * widened, axis=1)), MX)
    average = totals[0][:, None] / width
    spread = totals[1][:, None] / width - average * average
    inv_scale = lax.rsqrt(spread + epsilon)
    normed = (widened - average) * inv_scale
    scaled = (normed * ln_gain[None, :]).astype(jnp.bfloat16)
    local_heads = qk_gain.shape[1]
    head_size = qk_gain.shape[2]
    group_heads = w_qkv.shape[2] // head_size
    weights = w_qkv.reshape(3, width_local, group_heads, head_size)
    n_x = lax.axis_size("mxx")
    n_c = lax.axis_size("mxc")
    ordered = w_qkv.reshape(3, width_local, n_x, n_c, local_heads, head_size)
    partial = jnp.einsum("td,sdabje->bajste", scaled, ordered, preferred_element_type=jnp.float32)
    on_chip = jnp.sum(lax.all_to_all(partial, "mxc", split_axis=0, concat_axis=0), axis=0)
    projected = jnp.sum(lax.all_to_all(on_chip, "mxx", split_axis=0, concat_axis=0), axis=0)
    projected = projected.astype(jnp.bfloat16)
    images = token_rows // PATCH
    shaped = projected.reshape(local_heads, 3, images, PATCH, head_size)
    q_hat, q_inv = head_norm(shaped[:, 0].astype(jnp.float32))
    k_hat, k_inv = head_norm(shaped[:, 1].astype(jnp.float32))
    values = shaped[:, 2]
    q_gain = qk_gain[0][:, None, None, :]
    k_gain = qk_gain[1][:, None, None, :]
    q_normed = (q_hat * q_gain).astype(jnp.bfloat16)
    k_normed = (k_hat * k_gain).astype(jnp.bfloat16)
    factor = 1.0 / math.sqrt(head_size)
    scores = (
        jnp.einsum("hipe,hiqe->hipq", q_normed, k_normed, preferred_element_type=jnp.float32)
        * factor
    )
    row_max = jnp.max(scores, axis=-1, keepdims=True)
    exponent = jnp.exp(scores - row_max)
    probabilities = exponent / jnp.sum(exponent, axis=-1, keepdims=True)
    probs_low = probabilities.astype(jnp.bfloat16)
    grad_heads = (
        d_out.reshape(token_rows, local_heads, head_size)
        .transpose(1, 0, 2)
        .reshape(local_heads, images, PATCH, head_size)
    )
    d_values = jnp.einsum(
        "hipq,hipe->hiqe", probs_low, grad_heads, preferred_element_type=jnp.float32
    ).astype(jnp.bfloat16)
    d_probs = jnp.einsum("hipe,hiqe->hipq", grad_heads, values, preferred_element_type=jnp.float32)
    row_delta = jnp.sum(probabilities * d_probs, axis=-1, keepdims=True)
    d_scores = (probabilities * (d_probs - row_delta) * factor).astype(jnp.bfloat16)
    d_qn = jnp.einsum("hipq,hiqe->hipe", d_scores, k_normed, preferred_element_type=jnp.float32)
    d_kn = jnp.einsum("hipq,hipe->hiqe", d_scores, q_normed, preferred_element_type=jnp.float32)
    head_gain_part = jnp.stack(
        [jnp.sum(d_qn * q_hat, axis=(1, 2)), jnp.sum(d_kn * k_hat, axis=(1, 2))]
    )
    d_query = norm_back(d_qn, q_hat, q_inv, q_gain).astype(jnp.bfloat16)
    d_key = norm_back(d_kn, k_hat, k_inv, k_gain).astype(jnp.bfloat16)

    def head_rows(grads):
        return grads.reshape(local_heads, token_rows, head_size)

    block_rows = width_local // (lax.axis_size("dph") * lax.axis_size("dpz"))
    stacked = jnp.stack([head_rows(d_query), head_rows(d_key), head_rows(d_values)], axis=1)
    gathered = lax.all_gather(stacked, MX, axis=0, tiled=True)
    d_scaled = jnp.einsum("hste,sdhe->td", gathered, weights, preferred_element_type=jnp.float32)
    feature_part = scaled
    n_hi = lax.axis_size("dph")
    n_z = lax.axis_size("dpz")
    feature_part = (
        feature_part.reshape(token_rows, n_hi, n_z, -1).transpose(0, 2, 1, 3).reshape(token_rows, -1)
    )
    w_part = jnp.einsum(
        "td,hste->dshe", feature_part, gathered, preferred_element_type=jnp.float32
    ).astype(jnp.bfloat16)
    w_half = lax.psum_scatter(w_part, "dpz", scatter_dimension=0, tiled=True)
    gain_row = ln_gain[None, :]
    d_low = d_scaled.astype(jnp.bfloat16)
    d_other = lax.ppermute(d_low, "my", [(0, 1), (1, 0)])
    d_rows = d_low.astype(jnp.float32) + d_other.astype(jnp.float32)
    d_hat = d_rows * gain_row
    stat_sums = lax.psum((jnp.sum(d_hat, axis=1), jnp.sum(d_hat * normed, axis=1)), MX)
    sum_first = stat_sums[0]
    sum_second = stat_sums[1]
    result_rows = (
        inv_scale * (d_hat - sum_first[:, None] / width - normed * sum_second[:, None] / width)
    ).astype(jnp.bfloat16)
    feature_part = jnp.sum(d_rows * normed, axis=0)
    head_total, feature_total = lax.psum((head_gain_part, feature_part), ("dph", "dpz"))
    w_half, result_rows, feature_total, head_total = lax.optimization_barrier(
        (w_half, result_rows, feature_total, head_total)
    )
    w_rows = lax.psum_scatter(w_half, "dph", scatter_dimension=0, tiled=True).astype(jnp.float32)
    w_grad = (
        w_rows.reshape(block_rows, 3, group_heads * head_size)
        .transpose(1, 0, 2)
        .astype(jnp.bfloat16)
    )
    return (result_rows, w_grad, feature_total, head_total)


def solution(mesh):
    dp = ("dph", "dpz")
    devices = mesh.devices.reshape(2, mesh.shape["dp"] // 2, mesh.shape["mx"] // 2, 2, mesh.shape["my"])
    split_mesh = jax.sharding.Mesh(devices, ("dph", "dpz") + MX + ("my",))
    in_specs = (
        P(dp, MX),
        P(MX),
        P(None, MX, "my"),
        P(None, ("my",) + MX, None),
        P(dp, ("my",) + MX),
    )
    out_specs = (P(dp, MX), P(None, MX + dp, "my"), P(MX), P(None, ("my",) + MX, None))
    return jax.shard_map(body, mesh=split_mesh, in_specs=in_specs, out_specs=out_specs, check_vma=False)
```

```python
import math

import jax
import jax.numpy as jnp
from jax import lax
from jax.sharding import PartitionSpec as P

PATCH = 256
MX = ("mxx", "mxc")


epsilon = 1e-06


def head_norm(values):
    average = jnp.mean(values, axis=-1, keepdims=True)
    spread = jnp.mean(values * values, axis=-1, keepdims=True) - average * average
    inv_scale = lax.rsqrt(spread + epsilon)
    return ((values - average) * inv_scale, inv_scale)


def norm_back(d_normed, normed, inv_scale, gain_row):
    d_hat = d_normed * gain_row
    return inv_scale * (
        d_hat
        - jnp.mean(d_hat, axis=-1, keepdims=True)
        - normed * jnp.mean(d_hat * normed, axis=-1, keepdims=True)
    )


def body(inputs, ln_gain, w_qkv, qk_gain, d_out):
    token_rows = inputs.shape[0]
    width_local = inputs.shape[1]
    width = width_local * lax.axis_size(MX)
    widened = inputs.astype(jnp.float32)
    totals = lax.psum((jnp.sum(widened, axis=1), jnp.sum(widened * widened, axis=1)), MX)
    average = totals[0][:, None] / width
    spread = totals[1][:, None] / width - average * average
    inv_scale = lax.rsqrt(spread + epsilon)
    normed = (widened - average) * inv_scale
    scaled = (normed * ln_gain[None, :]).astype(jnp.bfloat16)
    local_heads = qk_gain.shape[1]
    head_size = qk_gain.shape[2]
    group_heads = w_qkv.shape[2] // head_size
    weights = w_qkv.reshape(3, width_local, group_heads, head_size)
    n_x = lax.axis_size("mxx")
    n_c = lax.axis_size("mxc")
    partial = jnp.einsum("td,sdhe->hste", scaled, weights, preferred_element_type=jnp.float32)
    partial = partial.reshape(n_x, n_c, local_heads, 3, token_rows, head_size).transpose(1, 0, 2, 3, 4, 5)
    on_chip = jnp.sum(lax.all_to_all(partial, "mxc", split_axis=0, concat_axis=0), axis=0)
    projected = jnp.sum(lax.all_to_all(on_chip, "mxx", split_axis=0, concat_axis=0), axis=0)
    projected = projected.astype(jnp.bfloat16)
    images = token_rows // PATCH
    shaped = projected.reshape(local_heads, 3, images, PATCH, head_size)
    q_hat, q_inv = head_norm(shaped[:, 0].astype(jnp.float32))
    k_hat, k_inv = head_norm(shaped[:, 1].astype(jnp.float32))
    values = shaped[:, 2]
    q_gain = qk_gain[0][:, None, None, :]
    k_gain = qk_gain[1][:, None, None, :]
    q_normed = (q_hat * q_gain).astype(jnp.bfloat16)
    k_normed = (k_hat * k_gain).astype(jnp.bfloat16)
    factor = 1.0 / math.sqrt(head_size)
    scores = (
        jnp.einsum("hipe,hiqe->hipq", q_normed, k_normed, preferred_element_type=jnp.float32)
        * factor
    )
    row_max = jnp.max(scores, axis=-1, keepdims=True)
    exponent = jnp.exp(scores - row_max)
    probabilities = exponent / jnp.sum(exponent, axis=-1, keepdims=True)
    probs_low = probabilities.astype(jnp.bfloat16)
    grad_heads = (
        d_out.reshape(token_rows, local_heads, head_size)
        .transpose(1, 0, 2)
        .reshape(local_heads, images, PATCH, head_size)
    )
    d_values = jnp.einsum(
        "hipq,hipe->hiqe", probs_low, grad_heads, preferred_element_type=jnp.float32
    ).astype(jnp.bfloat16)
    d_probs = jnp.einsum("hipe,hiqe->hipq", grad_heads, values, preferred_element_type=jnp.float32)
    row_delta = jnp.sum(probabilities * d_probs, axis=-1, keepdims=True)
    d_scores = (probabilities * (d_probs - row_delta) * factor).astype(jnp.bfloat16)
    d_qn = jnp.einsum("hipq,hiqe->hipe", d_scores, k_normed, preferred_element_type=jnp.float32)
    d_kn = jnp.einsum("hipq,hipe->hiqe", d_scores, q_normed, preferred_element_type=jnp.float32)
    head_gain_part = jnp.stack(
        [jnp.sum(d_qn * q_hat, axis=(1, 2)), jnp.sum(d_kn * k_hat, axis=(1, 2))]
    )
    d_query = norm_back(d_qn, q_hat, q_inv, q_gain).astype(jnp.bfloat16)
    d_key = norm_back(d_kn, k_hat, k_inv, k_gain).astype(jnp.bfloat16)

    def head_rows(grads):
        return grads.reshape(local_heads, token_rows, head_size)

    block_rows = width_local // (lax.axis_size("dph") * lax.axis_size("dpz"))
    stacked = jnp.stack([head_rows(d_query), head_rows(d_key), head_rows(d_values)], axis=1)
    gathered = lax.all_gather(stacked, MX, axis=0, tiled=True)
    d_scaled = jnp.einsum("hste,sdhe->td", gathered, weights, preferred_element_type=jnp.float32)
    feature_part = scaled
    n_hi = lax.axis_size("dph")
    n_z = lax.axis_size("dpz")
    feature_part = (
        feature_part.reshape(token_rows, n_hi, n_z, -1).transpose(0, 2, 1, 3).reshape(token_rows, -1)
    )
    w_part = jnp.einsum(
        "td,hste->dshe", feature_part, gathered, preferred_element_type=jnp.float32
    ).astype(jnp.bfloat16)
    w_half = lax.psum_scatter(w_part, "dpz", scatter_dimension=0, tiled=True)
    gain_row = ln_gain[None, :]
    d_low = d_scaled.astype(jnp.bfloat16)
    d_other = lax.ppermute(d_low, "my", [(0, 1), (1, 0)])
    d_rows = d_low.astype(jnp.float32) + d_other.astype(jnp.float32)
    d_hat = d_rows * gain_row
    stat_sums = lax.psum((jnp.sum(d_hat, axis=1), jnp.sum(d_hat * normed, axis=1)), MX)
    sum_first = stat_sums[0]
    sum_second = stat_sums[1]
    result_rows = (
        inv_scale * (d_hat - sum_first[:, None] / width - normed * sum_second[:, None] / width)
    ).astype(jnp.bfloat16)
    feature_part = jnp.sum(d_rows * normed, axis=0)
    head_total, feature_total = lax.psum((head_gain_part, feature_part), ("dph", "dpz"))
    w_half, result_rows, feature_total, head_total = lax.optimization_barrier(
        (w_half, result_rows, feature_total, head_total)
    )
    w_rows = lax.psum_scatter(w_half, "dph", scatter_dimension=0, tiled=True).astype(jnp.float32)
    w_grad = (
        w_rows.reshape(block_rows, 3, group_heads * head_size)
        .transpose(1, 0, 2)
        .astype(jnp.bfloat16)
    )
    return (result_rows, w_grad, feature_total, head_total)


def solution(mesh):
    dp = ("dph", "dpz")
    devices = mesh.devices.reshape(2, mesh.shape["dp"] // 2, mesh.shape["mx"] // 2, 2, mesh.shape["my"])
    split_mesh = jax.sharding.Mesh(devices, ("dph", "dpz") + MX + ("my",))
    in_specs = (
        P(dp, MX),
        P(MX),
        P(None, MX, "my"),
        P(None, ("my",) + MX, None),
        P(dp, ("my",) + MX),
    )
    out_specs = (P(dp, MX), P(None, MX + dp, "my"), P(MX), P(None, ("my",) + MX, None))
    return jax.shard_map(body, mesh=split_mesh, in_specs=in_specs, out_specs=out_specs, check_vma=False)
```

```python
import math

import jax
import jax.numpy as jnp
from jax import lax
from jax.sharding import PartitionSpec as P

PATCH = 256
MX = ("mxx", "mxc")


epsilon = 1e-06


def head_norm(values):
    average = jnp.mean(values, axis=-1, keepdims=True)
    spread = jnp.mean(values * values, axis=-1, keepdims=True) - average * average
    inv_scale = lax.rsqrt(spread + epsilon)
    return ((values - average) * inv_scale, inv_scale)


def norm_back(d_normed, normed, inv_scale, gain_row):
    d_hat = d_normed * gain_row
    return inv_scale * (
        d_hat
        - jnp.mean(d_hat, axis=-1, keepdims=True)
        - normed * jnp.mean(d_hat * normed, axis=-1, keepdims=True)
    )


def body(inputs, ln_gain, w_qkv, qk_gain, d_out):
    token_rows = inputs.shape[0]
    width_local = inputs.shape[1]
    width = width_local * lax.axis_size(MX)
    widened = inputs.astype(jnp.float32)
    totals = lax.psum((jnp.sum(widened, axis=1), jnp.sum(widened * widened, axis=1)), MX)
    average = totals[0][:, None] / width
    spread = totals[1][:, None] / width - average * average
    inv_scale = lax.rsqrt(spread + epsilon)
    normed = (widened - average) * inv_scale
    scaled = (normed * ln_gain[None, :]).astype(jnp.bfloat16)
    local_heads = qk_gain.shape[1]
    head_size = qk_gain.shape[2]
    group_heads = w_qkv.shape[2] // head_size
    weights = w_qkv.reshape(3, width_local, group_heads, head_size)
    n_x = lax.axis_size("mxx")
    n_c = lax.axis_size("mxc")
    partial = jnp.einsum("td,sdhe->hste", scaled, weights, preferred_element_type=jnp.float32)
    partial = partial.reshape(n_x, n_c, local_heads, 3, token_rows, head_size).transpose(1, 0, 2, 3, 4, 5)
    on_chip = jnp.sum(lax.all_to_all(partial, "mxc", split_axis=0, concat_axis=0), axis=0)
    projected = jnp.sum(lax.all_to_all(on_chip, "mxx", split_axis=0, concat_axis=0), axis=0)
    projected = projected.astype(jnp.bfloat16)
    images = token_rows // PATCH
    shaped = projected.reshape(local_heads, 3, images, PATCH, head_size)
    q_hat, q_inv = head_norm(shaped[:, 0].astype(jnp.float32))
    k_hat, k_inv = head_norm(shaped[:, 1].astype(jnp.float32))
    values = shaped[:, 2]
    q_gain = qk_gain[0][:, None, None, :]
    k_gain = qk_gain[1][:, None, None, :]
    q_normed = (q_hat * q_gain).astype(jnp.bfloat16)
    k_normed = (k_hat * k_gain).astype(jnp.bfloat16)
    factor = 1.0 / math.sqrt(head_size)
    scores = (
        jnp.einsum("hipe,hiqe->hipq", q_normed, k_normed, preferred_element_type=jnp.float32)
        * factor
    )
    row_max = jnp.max(scores, axis=-1, keepdims=True)
    exponent = jnp.exp(scores - row_max)
    probabilities = exponent / jnp.sum(exponent, axis=-1, keepdims=True)
    probs_low = probabilities.astype(jnp.bfloat16)
    grad_heads = (
        d_out.reshape(token_rows, local_heads, head_size)
        .transpose(1, 0, 2)
        .reshape(local_heads, images, PATCH, head_size)
    )
    d_values = jnp.einsum(
        "hipq,hipe->hiqe", probs_low, grad_heads, preferred_element_type=jnp.float32
    ).astype(jnp.bfloat16)
    d_probs = jnp.einsum("hipe,hiqe->hipq", grad_heads, values, preferred_element_type=jnp.float32)
    row_delta = jnp.sum(probabilities * d_probs, axis=-1, keepdims=True)
    d_scores = (probabilities * (d_probs - row_delta) * factor).astype(jnp.bfloat16)
    d_qn = jnp.einsum("hipq,hiqe->hipe", d_scores, k_normed, preferred_element_type=jnp.float32)
    d_kn = jnp.einsum("hipq,hipe->hiqe", d_scores, q_normed, preferred_element_type=jnp.float32)
    head_gain_part = jnp.stack(
        [jnp.sum(d_qn * q_hat, axis=(1, 2)), jnp.sum(d_kn * k_hat, axis=(1, 2))]
    )
    d_query = norm_back(d_qn, q_hat, q_inv, q_gain).astype(jnp.bfloat16)
    d_key = norm_back(d_kn, k_hat, k_inv, k_gain).astype(jnp.bfloat16)

    def head_rows(grads):
        return grads.reshape(local_heads, token_rows, head_size)

    block_rows = width_local // (lax.axis_size("dph") * lax.axis_size("dpz"))
    stacked = jnp.stack([head_rows(d_query), head_rows(d_key), head_rows(d_values)], axis=1)
    across = lax.all_gather(stacked, "mxx", axis=0, tiled=False)
    paired = lax.all_gather(across, "mxc", axis=0, tiled=False)
    gathered = paired.transpose(1, 0, *range(2, paired.ndim)).reshape((-1,) + stacked.shape[1:])
    d_scaled = jnp.einsum("hste,sdhe->td", gathered, weights, preferred_element_type=jnp.float32)
    feature_part = scaled
    n_hi = lax.axis_size("dph")
    n_z = lax.axis_size("dpz")
    feature_part = (
        feature_part.reshape(token_rows, n_hi, n_z, -1).transpose(0, 2, 1, 3).reshape(token_rows, -1)
    )
    w_part = jnp.einsum(
        "td,hste->dshe", feature_part, gathered, preferred_element_type=jnp.float32
    ).astype(jnp.bfloat16)
    w_half = lax.psum_scatter(w_part, "dpz", scatter_dimension=0, tiled=True)
    gain_row = ln_gain[None, :]
    d_low = d_scaled.astype(jnp.bfloat16)
    d_other = lax.ppermute(d_low, "my", [(0, 1), (1, 0)])
    d_rows = d_low.astype(jnp.float32) + d_other.astype(jnp.float32)
    d_hat = d_rows * gain_row
    stat_sums = lax.psum((jnp.sum(d_hat, axis=1), jnp.sum(d_hat * normed, axis=1)), MX)
    sum_first = stat_sums[0]
    sum_second = stat_sums[1]
    result_rows = (
        inv_scale * (d_hat - sum_first[:, None] / width - normed * sum_second[:, None] / width)
    ).astype(jnp.bfloat16)
    feature_part = jnp.sum(d_rows * normed, axis=0)
    head_total, feature_total = lax.psum((head_gain_part, feature_part), ("dph", "dpz"))
    w_half, result_rows, feature_total, head_total = lax.optimization_barrier(
        (w_half, result_rows, feature_total, head_total)
    )
    w_rows = lax.psum_scatter(w_half, "dph", scatter_dimension=0, tiled=True).astype(jnp.float32)
    w_grad = (
        w_rows.reshape(block_rows, 3, group_heads * head_size)
        .transpose(1, 0, 2)
        .astype(jnp.bfloat16)
    )
    return (result_rows, w_grad, feature_total, head_total)


def solution(mesh):
    dp = ("dph", "dpz")
    devices = mesh.devices.reshape(2, mesh.shape["dp"] // 2, mesh.shape["mx"] // 2, 2, mesh.shape["my"])
    split_mesh = jax.sharding.Mesh(devices, ("dph", "dpz") + MX + ("my",))
    in_specs = (
        P(dp, MX),
        P(MX),
        P(None, MX, "my"),
        P(None, ("my",) + MX, None),
        P(dp, ("my",) + MX),
    )
    out_specs = (P(dp, MX), P(None, MX + dp, "my"), P(MX), P(None, ("my",) + MX, None))
    return jax.shard_map(body, mesh=split_mesh, in_specs=in_specs, out_specs=out_specs, check_vma=False)
```

```python
import math

import jax
import jax.numpy as jnp
from jax import lax
from jax.sharding import PartitionSpec as P

PATCH = 256
MX = ("mxx", "mxc")


epsilon = 1e-06


def head_norm(values):
    average = jnp.mean(values, axis=-1, keepdims=True)
    spread = jnp.mean(values * values, axis=-1, keepdims=True) - average * average
    inv_scale = lax.rsqrt(spread + epsilon)
    return ((values - average) * inv_scale, inv_scale)


def norm_back(d_normed, normed, inv_scale, gain_row):
    d_hat = d_normed * gain_row
    return inv_scale * (
        d_hat
        - jnp.mean(d_hat, axis=-1, keepdims=True)
        - normed * jnp.mean(d_hat * normed, axis=-1, keepdims=True)
    )


def body(inputs, ln_gain, w_qkv, qk_gain, d_out):
    token_rows = inputs.shape[0]
    width_local = inputs.shape[1]
    width = width_local * lax.axis_size(MX)
    widened = inputs.astype(jnp.float32)
    totals = lax.psum((jnp.sum(widened, axis=1), jnp.sum(widened * widened, axis=1)), MX)
    average = totals[0][:, None] / width
    spread = totals[1][:, None] / width - average * average
    inv_scale = lax.rsqrt(spread + epsilon)
    normed = (widened - average) * inv_scale
    scaled = (normed * ln_gain[None, :]).astype(jnp.bfloat16)
    local_heads = qk_gain.shape[1]
    head_size = qk_gain.shape[2]
    group_heads = w_qkv.shape[2] // head_size
    weights = w_qkv.reshape(3, width_local, group_heads, head_size)
    n_x = lax.axis_size("mxx")
    n_c = lax.axis_size("mxc")
    partial = jnp.einsum("td,sdhe->hste", scaled, weights, preferred_element_type=jnp.float32)
    partial = partial.reshape(n_x, n_c, local_heads, 3, token_rows, head_size).transpose(1, 0, 2, 3, 4, 5)
    on_chip = jnp.sum(lax.all_to_all(partial, "mxc", split_axis=0, concat_axis=0), axis=0)
    projected = jnp.sum(lax.all_to_all(on_chip, "mxx", split_axis=0, concat_axis=0), axis=0)
    projected = projected.astype(jnp.bfloat16)
    images = token_rows // PATCH
    shaped = projected.reshape(local_heads, 3, images, PATCH, head_size)
    q_hat, q_inv = head_norm(shaped[:, 0].astype(jnp.float32))
    k_hat, k_inv = head_norm(shaped[:, 1].astype(jnp.float32))
    values = shaped[:, 2]
    q_gain = qk_gain[0][:, None, None, :]
    k_gain = qk_gain[1][:, None, None, :]
    q_normed = (q_hat * q_gain).astype(jnp.bfloat16)
    k_normed = (k_hat * k_gain).astype(jnp.bfloat16)
    factor = 1.0 / math.sqrt(head_size)
    scores = (
        jnp.einsum("hipe,hiqe->hipq", q_normed, k_normed, preferred_element_type=jnp.float32)
        * factor
    )
    row_max = jnp.max(scores, axis=-1, keepdims=True)
    exponent = jnp.exp(scores - row_max)
    probabilities = exponent / jnp.sum(exponent, axis=-1, keepdims=True)
    probs_low = probabilities.astype(jnp.bfloat16)
    grad_heads = (
        d_out.reshape(token_rows, local_heads, head_size)
        .transpose(1, 0, 2)
        .reshape(local_heads, images, PATCH, head_size)
    )
    d_values = jnp.einsum(
        "hipq,hipe->hiqe", probs_low, grad_heads, preferred_element_type=jnp.float32
    ).astype(jnp.bfloat16)
    d_probs = jnp.einsum("hipe,hiqe->hipq", grad_heads, values, preferred_element_type=jnp.float32)
    row_delta = jnp.sum(probabilities * d_probs, axis=-1, keepdims=True)
    d_scores = (probabilities * (d_probs - row_delta) * factor).astype(jnp.bfloat16)
    d_qn = jnp.einsum("hipq,hiqe->hipe", d_scores, k_normed, preferred_element_type=jnp.float32)
    d_kn = jnp.einsum("hipq,hipe->hiqe", d_scores, q_normed, preferred_element_type=jnp.float32)
    head_gain_part = jnp.stack(
        [jnp.sum(d_qn * q_hat, axis=(1, 2)), jnp.sum(d_kn * k_hat, axis=(1, 2))]
    )
    d_query = norm_back(d_qn, q_hat, q_inv, q_gain).astype(jnp.bfloat16)
    d_key = norm_back(d_kn, k_hat, k_inv, k_gain).astype(jnp.bfloat16)

    def head_rows(grads):
        return grads.reshape(local_heads, token_rows, head_size)

    block_rows = width_local // (lax.axis_size("dph") * lax.axis_size("dpz"))
    stacked = jnp.stack([head_rows(d_query), head_rows(d_key), head_rows(d_values)], axis=1)
    gathered = lax.all_gather(stacked, MX, axis=0, tiled=True)
    d_scaled = jnp.einsum("hste,sdhe->td", gathered, weights, preferred_element_type=jnp.float32)
    feature_part = scaled
    n_hi = lax.axis_size("dph")
    n_z = lax.axis_size("dpz")
    feature_part = (
        feature_part.reshape(token_rows, n_hi, n_z, -1).transpose(0, 2, 1, 3).reshape(token_rows, -1)
    )
    w_part = jnp.einsum(
        "td,hste->dshe", feature_part, gathered, preferred_element_type=jnp.float32
    ).astype(jnp.bfloat16)
    w_half = lax.psum_scatter(w_part, "dpz", scatter_dimension=0, tiled=True)
    gain_row = ln_gain[None, :]
    d_low = d_scaled.astype(jnp.bfloat16)
    d_other = lax.ppermute(d_low, "my", [(0, 1), (1, 0)])
    d_rows = d_low.astype(jnp.float32) + d_other.astype(jnp.float32)
    d_hat = d_rows * gain_row
    stat_sums = lax.psum((jnp.sum(d_hat, axis=1), jnp.sum(d_hat * normed, axis=1)), MX)
    sum_first = stat_sums[0]
    sum_second = stat_sums[1]
    result_rows = (
        inv_scale * (d_hat - sum_first[:, None] / width - normed * sum_second[:, None] / width)
    ).astype(jnp.bfloat16)
    feature_part = jnp.sum(d_rows * normed, axis=0)
    head_total, feature_total = lax.psum((head_gain_part, feature_part), ("dph", "dpz"))
    w_half, result_rows, feature_total, head_total = lax.optimization_barrier(
        (w_half, result_rows, feature_total, head_total)
    )
    hi_index = lax.axis_index("dph")
    halves = w_half.reshape((n_hi, -1) + w_half.shape[1:])
    swapped = lax.ppermute(halves[1 - hi_index], "dph", [(0, 1), (1, 0)])
    w_rows = halves[hi_index].astype(jnp.float32) + swapped.astype(jnp.float32)
    w_grad = (
        w_rows.reshape(block_rows, 3, group_heads * head_size)
        .transpose(1, 0, 2)
        .astype(jnp.bfloat16)
    )
    return (result_rows, w_grad, feature_total, head_total)


def solution(mesh):
    dp = ("dph", "dpz")
    devices = mesh.devices.reshape(2, mesh.shape["dp"] // 2, mesh.shape["mx"] // 2, 2, mesh.shape["my"])
    split_mesh = jax.sharding.Mesh(devices, ("dph", "dpz") + MX + ("my",))
    in_specs = (
        P(dp, MX),
        P(MX),
        P(None, MX, "my"),
        P(None, ("my",) + MX, None),
        P(dp, ("my",) + MX),
    )
    out_specs = (P(dp, MX), P(None, MX + dp, "my"), P(MX), P(None, ("my",) + MX, None))
    return jax.shard_map(body, mesh=split_mesh, in_specs=in_specs, out_specs=out_specs, check_vma=False)
```

```python
import math

import jax
import jax.numpy as jnp
from jax import lax
from jax.sharding import PartitionSpec as P

PATCH = 256
MX = ("mxx", "mxc")


epsilon = 1e-06


def head_norm(values):
    average = jnp.mean(values, axis=-1, keepdims=True)
    spread = jnp.mean(values * values, axis=-1, keepdims=True) - average * average
    inv_scale = lax.rsqrt(spread + epsilon)
    return ((values - average) * inv_scale, inv_scale)


def norm_back(d_normed, normed, inv_scale, gain_row):
    d_hat = d_normed * gain_row
    return inv_scale * (
        d_hat
        - jnp.mean(d_hat, axis=-1, keepdims=True)
        - normed * jnp.mean(d_hat * normed, axis=-1, keepdims=True)
    )


def body(inputs, ln_gain, w_qkv, qk_gain, d_out):
    token_rows = inputs.shape[0]
    width_local = inputs.shape[1]
    width = width_local * lax.axis_size(MX)
    widened = inputs.astype(jnp.float32)
    totals = lax.psum((jnp.sum(widened, axis=1), jnp.sum(widened * widened, axis=1)), "mxc")
    totals = lax.psum(totals, "mxx")
    average = totals[0][:, None] / width
    spread = totals[1][:, None] / width - average * average
    inv_scale = lax.rsqrt(spread + epsilon)
    normed = (widened - average) * inv_scale
    scaled = (normed * ln_gain[None, :]).astype(jnp.bfloat16)
    local_heads = qk_gain.shape[1]
    head_size = qk_gain.shape[2]
    group_heads = w_qkv.shape[2] // head_size
    weights = w_qkv.reshape(3, width_local, group_heads, head_size)
    n_x = lax.axis_size("mxx")
    n_c = lax.axis_size("mxc")
    partial = jnp.einsum("td,sdhe->hste", scaled, weights, preferred_element_type=jnp.float32)
    partial = partial.reshape(n_x, n_c, local_heads, 3, token_rows, head_size).transpose(1, 0, 2, 3, 4, 5)
    on_chip = jnp.sum(lax.all_to_all(partial, "mxc", split_axis=0, concat_axis=0), axis=0)
    projected = jnp.sum(lax.all_to_all(on_chip, "mxx", split_axis=0, concat_axis=0), axis=0)
    projected = projected.astype(jnp.bfloat16)
    images = token_rows // PATCH
    shaped = projected.reshape(local_heads, 3, images, PATCH, head_size)
    q_hat, q_inv = head_norm(shaped[:, 0].astype(jnp.float32))
    k_hat, k_inv = head_norm(shaped[:, 1].astype(jnp.float32))
    values = shaped[:, 2]
    q_gain = qk_gain[0][:, None, None, :]
    k_gain = qk_gain[1][:, None, None, :]
    q_normed = (q_hat * q_gain).astype(jnp.bfloat16)
    k_normed = (k_hat * k_gain).astype(jnp.bfloat16)
    factor = 1.0 / math.sqrt(head_size)
    scores = (
        jnp.einsum("hipe,hiqe->hipq", q_normed, k_normed, preferred_element_type=jnp.float32)
        * factor
    )
    row_max = jnp.max(scores, axis=-1, keepdims=True)
    exponent = jnp.exp(scores - row_max)
    probabilities = exponent / jnp.sum(exponent, axis=-1, keepdims=True)
    probs_low = probabilities.astype(jnp.bfloat16)
    grad_heads = (
        d_out.reshape(token_rows, local_heads, head_size)
        .transpose(1, 0, 2)
        .reshape(local_heads, images, PATCH, head_size)
    )
    d_values = jnp.einsum(
        "hipq,hipe->hiqe", probs_low, grad_heads, preferred_element_type=jnp.float32
    ).astype(jnp.bfloat16)
    d_probs = jnp.einsum("hipe,hiqe->hipq", grad_heads, values, preferred_element_type=jnp.float32)
    row_delta = jnp.sum(probabilities * d_probs, axis=-1, keepdims=True)
    d_scores = (probabilities * (d_probs - row_delta) * factor).astype(jnp.bfloat16)
    d_qn = jnp.einsum("hipq,hiqe->hipe", d_scores, k_normed, preferred_element_type=jnp.float32)
    d_kn = jnp.einsum("hipq,hipe->hiqe", d_scores, q_normed, preferred_element_type=jnp.float32)
    head_gain_part = jnp.stack(
        [jnp.sum(d_qn * q_hat, axis=(1, 2)), jnp.sum(d_kn * k_hat, axis=(1, 2))]
    )
    d_query = norm_back(d_qn, q_hat, q_inv, q_gain).astype(jnp.bfloat16)
    d_key = norm_back(d_kn, k_hat, k_inv, k_gain).astype(jnp.bfloat16)

    def head_rows(grads):
        return grads.reshape(local_heads, token_rows, head_size)

    block_rows = width_local // (lax.axis_size("dph") * lax.axis_size("dpz"))
    stacked = jnp.stack([head_rows(d_query), head_rows(d_key), head_rows(d_values)], axis=1)
    gathered = lax.all_gather(stacked, MX, axis=0, tiled=True)
    d_scaled = jnp.einsum("hste,sdhe->td", gathered, weights, preferred_element_type=jnp.float32)
    feature_part = scaled
    n_hi = lax.axis_size("dph")
    n_z = lax.axis_size("dpz")
    feature_part = (
        feature_part.reshape(token_rows, n_hi, n_z, -1).transpose(0, 2, 1, 3).reshape(token_rows, -1)
    )
    w_part = jnp.einsum(
        "td,hste->dshe", feature_part, gathered, preferred_element_type=jnp.float32
    ).astype(jnp.bfloat16)
    w_half = lax.psum_scatter(w_part, "dpz", scatter_dimension=0, tiled=True)
    gain_row = ln_gain[None, :]
    d_low = d_scaled.astype(jnp.bfloat16)
    d_other = lax.ppermute(d_low, "my", [(0, 1), (1, 0)])
    d_rows = d_low.astype(jnp.float32) + d_other.astype(jnp.float32)
    d_hat = d_rows * gain_row
    stat_sums = lax.psum((jnp.sum(d_hat, axis=1), jnp.sum(d_hat * normed, axis=1)), MX)
    sum_first = stat_sums[0]
    sum_second = stat_sums[1]
    result_rows = (
        inv_scale * (d_hat - sum_first[:, None] / width - normed * sum_second[:, None] / width)
    ).astype(jnp.bfloat16)
    feature_part = jnp.sum(d_rows * normed, axis=0)
    head_total, feature_total = lax.psum((head_gain_part, feature_part), ("dph", "dpz"))
    w_half, result_rows, feature_total, head_total = lax.optimization_barrier(
        (w_half, result_rows, feature_total, head_total)
    )
    hi_index = lax.axis_index("dph")
    halves = w_half.reshape((n_hi, -1) + w_half.shape[1:])
    swapped = lax.ppermute(halves[1 - hi_index], "dph", [(0, 1), (1, 0)])
    w_rows = halves[hi_index].astype(jnp.float32) + swapped.astype(jnp.float32)
    w_grad = (
        w_rows.reshape(block_rows, 3, group_heads * head_size)
        .transpose(1, 0, 2)
        .astype(jnp.bfloat16)
    )
    return (result_rows, w_grad, feature_total, head_total)


def solution(mesh):
    dp = ("dph", "dpz")
    devices = mesh.devices.reshape(2, mesh.shape["dp"] // 2, mesh.shape["mx"] // 2, 2, mesh.shape["my"])
    split_mesh = jax.sharding.Mesh(devices, ("dph", "dpz") + MX + ("my",))
    in_specs = (
        P(dp, MX),
        P(MX),
        P(None, MX, "my"),
        P(None, ("my",) + MX, None),
        P(dp, ("my",) + MX),
    )
    out_specs = (P(dp, MX), P(None, MX + dp, "my"), P(MX), P(None, ("my",) + MX, None))
    return jax.shard_map(body, mesh=split_mesh, in_specs=in_specs, out_specs=out_specs, check_vma=False)
```

```python
import math

import jax
import jax.numpy as jnp
from jax import lax
from jax.sharding import PartitionSpec as P

PATCH = 256
MX = ("mxx", "mxc")


epsilon = 1e-06


def head_norm(values):
    average = jnp.mean(values, axis=-1, keepdims=True)
    spread = jnp.mean(values * values, axis=-1, keepdims=True) - average * average
    inv_scale = lax.rsqrt(spread + epsilon)
    return ((values - average) * inv_scale, inv_scale)


def norm_back(d_normed, normed, inv_scale, gain_row):
    d_hat = d_normed * gain_row
    return inv_scale * (
        d_hat
        - jnp.mean(d_hat, axis=-1, keepdims=True)
        - normed * jnp.mean(d_hat * normed, axis=-1, keepdims=True)
    )


def body(inputs, ln_gain, w_qkv, qk_gain, d_out):
    token_rows = inputs.shape[0]
    width_local = inputs.shape[1]
    width = width_local * lax.axis_size(MX)
    widened = inputs.astype(jnp.float32)
    totals = lax.psum((jnp.sum(widened, axis=1), jnp.sum(widened * widened, axis=1)), "mxc")
    totals = lax.psum(totals, "mxx")
    average = totals[0][:, None] / width
    spread = totals[1][:, None] / width - average * average
    inv_scale = lax.rsqrt(spread + epsilon)
    normed = (widened - average) * inv_scale
    scaled = (normed * ln_gain[None, :]).astype(jnp.bfloat16)
    local_heads = qk_gain.shape[1]
    head_size = qk_gain.shape[2]
    group_heads = w_qkv.shape[2] // head_size
    weights = w_qkv.reshape(3, width_local, group_heads, head_size)
    n_x = lax.axis_size("mxx")
    n_c = lax.axis_size("mxc")
    partial = jnp.einsum("td,sdhe->hste", scaled, weights, preferred_element_type=jnp.float32)
    partial = partial.reshape(n_x, n_c, local_heads, 3, token_rows, head_size).transpose(1, 0, 2, 3, 4, 5)
    core_index = lax.axis_index("mxc")
    from_core = lax.ppermute(partial[1 - core_index], "mxc", [(0, 1), (1, 0)])
    on_chip = partial[core_index] + from_core
    projected = jnp.sum(lax.all_to_all(on_chip, "mxx", split_axis=0, concat_axis=0), axis=0)
    projected = projected.astype(jnp.bfloat16)
    images = token_rows // PATCH
    shaped = projected.reshape(local_heads, 3, images, PATCH, head_size)
    q_hat, q_inv = head_norm(shaped[:, 0].astype(jnp.float32))
    k_hat, k_inv = head_norm(shaped[:, 1].astype(jnp.float32))
    values = shaped[:, 2]
    q_gain = qk_gain[0][:, None, None, :]
    k_gain = qk_gain[1][:, None, None, :]
    q_normed = (q_hat * q_gain).astype(jnp.bfloat16)
    k_normed = (k_hat * k_gain).astype(jnp.bfloat16)
    factor = 1.0 / math.sqrt(head_size)
    scores = (
        jnp.einsum("hipe,hiqe->hipq", q_normed, k_normed, preferred_element_type=jnp.float32)
        * factor
    )
    row_max = jnp.max(scores, axis=-1, keepdims=True)
    exponent = jnp.exp(scores - row_max)
    probabilities = exponent / jnp.sum(exponent, axis=-1, keepdims=True)
    probs_low = probabilities.astype(jnp.bfloat16)
    grad_heads = (
        d_out.reshape(token_rows, local_heads, head_size)
        .transpose(1, 0, 2)
        .reshape(local_heads, images, PATCH, head_size)
    )
    d_values = jnp.einsum(
        "hipq,hipe->hiqe", probs_low, grad_heads, preferred_element_type=jnp.float32
    ).astype(jnp.bfloat16)
    d_probs = jnp.einsum("hipe,hiqe->hipq", grad_heads, values, preferred_element_type=jnp.float32)
    row_delta = jnp.sum(probabilities * d_probs, axis=-1, keepdims=True)
    d_scores = (probabilities * (d_probs - row_delta) * factor).astype(jnp.bfloat16)
    d_qn = jnp.einsum("hipq,hiqe->hipe", d_scores, k_normed, preferred_element_type=jnp.float32)
    d_kn = jnp.einsum("hipq,hipe->hiqe", d_scores, q_normed, preferred_element_type=jnp.float32)
    head_gain_part = jnp.stack(
        [jnp.sum(d_qn * q_hat, axis=(1, 2)), jnp.sum(d_kn * k_hat, axis=(1, 2))]
    )
    d_query = norm_back(d_qn, q_hat, q_inv, q_gain).astype(jnp.bfloat16)
    d_key = norm_back(d_kn, k_hat, k_inv, k_gain).astype(jnp.bfloat16)

    def head_rows(grads):
        return grads.reshape(local_heads, token_rows, head_size)

    block_rows = width_local // (lax.axis_size("dph") * lax.axis_size("dpz"))
    stacked = jnp.stack([head_rows(d_query), head_rows(d_key), head_rows(d_values)], axis=1)
    gathered = lax.all_gather(stacked, MX, axis=0, tiled=True)
    d_scaled = jnp.einsum("hste,sdhe->td", gathered, weights, preferred_element_type=jnp.float32)
    feature_part = scaled
    n_hi = lax.axis_size("dph")
    n_z = lax.axis_size("dpz")
    feature_part = (
        feature_part.reshape(token_rows, n_hi, n_z, -1).transpose(0, 2, 1, 3).reshape(token_rows, -1)
    )
    w_part = jnp.einsum(
        "td,hste->dshe", feature_part, gathered, preferred_element_type=jnp.float32
    ).astype(jnp.bfloat16)
    w_half = lax.psum_scatter(w_part, "dpz", scatter_dimension=0, tiled=True)
    gain_row = ln_gain[None, :]
    d_low = d_scaled.astype(jnp.bfloat16)
    d_other = lax.ppermute(d_low, "my", [(0, 1), (1, 0)])
    d_rows = d_low.astype(jnp.float32) + d_other.astype(jnp.float32)
    d_hat = d_rows * gain_row
    stat_sums = lax.psum((jnp.sum(d_hat, axis=1), jnp.sum(d_hat * normed, axis=1)), MX)
    sum_first = stat_sums[0]
    sum_second = stat_sums[1]
    result_rows = (
        inv_scale * (d_hat - sum_first[:, None] / width - normed * sum_second[:, None] / width)
    ).astype(jnp.bfloat16)
    feature_part = jnp.sum(d_rows * normed, axis=0)
    head_total, feature_total = lax.psum((head_gain_part, feature_part), ("dph", "dpz"))
    w_half, result_rows, feature_total, head_total = lax.optimization_barrier(
        (w_half, result_rows, feature_total, head_total)
    )
    hi_index = lax.axis_index("dph")
    halves = w_half.reshape((n_hi, -1) + w_half.shape[1:])
    swapped = lax.ppermute(halves[1 - hi_index], "dph", [(0, 1), (1, 0)])
    w_rows = halves[hi_index].astype(jnp.float32) + swapped.astype(jnp.float32)
    w_grad = (
        w_rows.reshape(block_rows, 3, group_heads * head_size)
        .transpose(1, 0, 2)
        .astype(jnp.bfloat16)
    )
    return (result_rows, w_grad, feature_total, head_total)


def solution(mesh):
    dp = ("dph", "dpz")
    devices = mesh.devices.reshape(2, mesh.shape["dp"] // 2, mesh.shape["mx"] // 2, 2, mesh.shape["my"])
    split_mesh = jax.sharding.Mesh(devices, ("dph", "dpz") + MX + ("my",))
    in_specs = (
        P(dp, MX),
        P(MX),
        P(None, MX, "my"),
        P(None, ("my",) + MX, None),
        P(dp, ("my",) + MX),
    )
    out_specs = (P(dp, MX), P(None, MX + dp, "my"), P(MX), P(None, ("my",) + MX, None))
    return jax.shard_map(body, mesh=split_mesh, in_specs=in_specs, out_specs=out_specs, check_vma=False)
```
